32 devices in a mesh: dp: 8 (over z, y), chan: 4 (over x, core).
Axes of the slice: x: 2, y: 2, z: 4, core: 2. Of those that a mesh axis runs over, the one named last changes fastest.
Arguments:
- activations: bfloat16 [8, 16, 64, 1024], P('dp', None, None, 'chan'), may hold values from -60 to 60
- cotangent: bfloat16 [8, 16, 64, 1024], P('dp', None, None, 'chan'), may hold values from -6 to 6
- dw_kernel: float32 [49, 1024], P(None, 'chan'), may hold values from -0.875 to 0.875
- norm_gain: float32 [4, 1024], P(None, 'chan'), may hold values from 0.1 to 1.9
- norm_bias: float32 [4, 1024], P(None, 'chan'), may hold values from -3 to 3
- w_in: bfloat16 [1024, 4096], P(None, 'chan'), may hold values from -0.1875 to 0.1875
- b_in: float32 [4096], P('chan'), may hold values from -3 to 3
- w_out: bfloat16 [4096, 1024], P('chan'), may hold values from -0.09375 to 0.09375
- layer_scale: float32 [1024], P('chan'), may hold values from 0.3 to 1.5
- group_sizes: int32 [4], replicated, may hold values from 1 to 4, 8 in all
Outputs:
- result: bfloat16 [8, 16, 64, 1024], P('dp', None, None, 'chan')
- d_input: bfloat16 [8, 16, 64, 1024], P('dp', None, None, 'chan')
- d_kernel: float32 [49, 1024], P(None, 'chan')
- d_gain: float32 [4, 1024], P(None, 'chan')
- d_bias: float32 [4, 1024], P(None, 'chan')
- d_w_in: float32 [1024, 4096], P('dp', 'chan')
- d_b_in: float32 [4096], P('chan')
- d_w_out: float32 [4096, 1024], P('chan', 'dp')
- d_scale: float32 [1024], P('chan')
The draws below stay inside these ranges and needn't reach their ends.
Inputs may be any that keep to these rules, and one draw needn't show every extreme that they name: `group_sizes`: the sizes sum to 8, each is at least one, and the largest is exactly 4.
All inputs are finite; a program needn't handle non-finite values.
Results may differ from the reference program's by a relative error of at most 0.015.
Values may be sent and summed in bfloat16 or wider, within the bound.
A program may use at most 128 MiB of HBM per device.

```python
import math
import jax
import jax.numpy as jnp
import numpy as np
from jax import lax

C = 1024
HID = 4096
KS = 7
IMG_H = 16
IMG_W = 64
GROUPS = 4
IMAGES = 8
N_DP = 8
N_CHAN = 4


def draw_activations(key, part):
    subkeys = jax.random.split(jax.random.fold_in(key, 17), 4)
    full_shape = (IMAGES, IMG_H, IMG_W, C)
    rising = 3.0 ** (jnp.arange(IMAGES, dtype=jnp.float32) / (IMAGES - 1))
    texture = jnp.exp(jax.random.uniform(subkeys[3], (1, IMG_H, IMG_W, 1), jnp.float32, -0.35, 0.35))
    values = jnp.clip(jax.random.normal(subkeys[0], full_shape, jnp.float32), -4.0, 4.0)
    spread = 0.3 * jnp.exp(jax.random.uniform(subkeys[1], (C,), jnp.float32, 0.0, math.log(10.0)))
    mixed = values * texture * spread * rising[:, None, None, None]
    return mixed.astype(jnp.bfloat16)


def level_of(rng, dims, cuts, low, top_value):
    level = 1.0
    for position, blocks in cuts:
        draws = jax.random.uniform(jax.random.fold_in(jax.random.fold_in(rng, 6), position), (blocks,), jnp.float32, low / len(cuts), top_value / len(cuts))
        level = level * jnp.repeat(jnp.exp(draws), dims[position] // blocks).reshape((-1,) + (1,) * (len(dims) - 1 - position))
    return level


def profile(amount, total, bound, lean):
    portions = [(1 << 20) // math.isqrt(standing ** lean) + 1 for standing in range(2, amount + 1)]
    spare, given = total - bound - (amount - 1), [1] * (amount - 1)
    while spare > 0:
        candidates = [i for i in range(amount - 1) if given[i] < bound]
        whole, budget = sum([portions[i] for i in candidates]), spare
        for i in candidates:
            more = min(bound - given[i], max(1, budget * portions[i] // whole), spare)
            given[i] = given[i] + more
            spare = spare - more
    return np.array([bound] + given)


def ragged_sizes(rng, number_of, total, limit, skew):
    if number_of == 2:
        one = jax.random.randint(rng, (), max(1, total - limit), min(limit, total - 1) + 1)
        return jnp.stack([one, total - one])
    tallies = jnp.asarray(profile(number_of, total, limit, skew), jnp.int32)
    twos = (number_of - 1) // 2
    source_of, taker = tallies[1:1 + 2 * twos:2], tallies[2:2 + 2 * twos:2]
    margin = jnp.minimum(source_of - 1, limit - taker)
    passed = jax.random.randint(jax.random.fold_in(rng, 1), (twos,), 0, 1 << 20) % (margin + 1)
    tallies = tallies.at[1:1 + 2 * twos:2].set(source_of - passed).at[2:2 + 2 * twos:2].set(taker + passed)
    return tallies[jax.random.permutation(jax.random.fold_in(rng, 2), number_of)]


def bell_draw(key, shape, scale, most, cuts=(), kind=jnp.bfloat16):
    drawn = scale * jax.random.normal(key, shape, jnp.float32)
    if cuts:
        drawn = drawn * level_of(key, shape, cuts, -0.22, 0.18)
    return jnp.clip(drawn, -most, most).astype(kind)


def setup_inputs(seed: int = 0) -> dict:
    arg_keys = jax.random.split(jax.random.key(seed), 11)
    activations = draw_activations(jax.random.fold_in(arg_keys[10], 71), 0)
    cotangent = bell_draw(arg_keys[1], (IMAGES, IMG_H, IMG_W, C), 1.0, 6.0, ((0, 8), (3, 4)))
    dw_kernel = bell_draw(arg_keys[2], (KS * KS, C), (KS * KS) ** -0.5, 0.875, ((1, 4),), jnp.float32)
    norm_gain = jnp.clip(1.0 + 0.18 * jax.random.normal(arg_keys[3], (GROUPS, C), jnp.float32), 0.1, 1.9)
    norm_bias = bell_draw(arg_keys[4], (GROUPS, C), 0.5, 3.0, ((1, 4),), jnp.float32)
    w_in = bell_draw(arg_keys[5], (C, HID), C ** -0.5, 0.1875, ((1, 4),))
    b_in = bell_draw(arg_keys[6], (HID,), 0.5, 3.0, ((0, 4),), jnp.float32)
    w_out = bell_draw(arg_keys[7], (HID, C), HID ** -0.5, 0.09375, ((0, 4),))
    layer_scale = jnp.clip(jnp.exp(math.log(1.5) - 1.60943787 * jax.random.uniform(arg_keys[8], (C,), jnp.float32) ** level_of(arg_keys[8], (C,), ((0, 4),), -0.2, 0.2)), 0.3, 1.5)
    group_sizes = ragged_sizes(arg_keys[9], GROUPS, N_DP, N_DP // 2, 2).astype(jnp.int32)
    return dict(activations=activations, cotangent=cotangent, dw_kernel=dw_kernel, norm_gain=norm_gain, norm_bias=norm_bias, w_in=w_in, b_in=b_in, w_out=w_out, layer_scale=layer_scale, group_sizes=group_sizes)


EPS = 1e-05

def depthwise(field, kernel):
    reach = KS // 2
    height, width = (field.shape[1], field.shape[2])
    padded = jnp.pad(field, ((0, 0), (reach, reach), (reach, reach), (0, 0)))
    running = jnp.zeros(field.shape, jnp.float32)
    for shift_row in range(KS):
        for shift_col in range(KS):
            window = padded[:, shift_row:shift_row + height, shift_col:shift_col + width, :]
            running = running + window * kernel[shift_row * KS + shift_col]
    return running

def kernel_grad(field, upstream):
    reach = KS // 2
    height, width = (field.shape[1], field.shape[2])
    padded = jnp.pad(field, ((0, 0), (reach, reach), (reach, reach), (0, 0)))
    collected = []
    for shift_row in range(KS):
        for shift_col in range(KS):
            window = padded[:, shift_row:shift_row + height, shift_col:shift_col + width, :]
            collected.append(lax.optimization_barrier(jnp.sum(window * upstream, axis=(0, 1, 2))))
    return jnp.stack(collected)

def group_member(group_sizes, number):
    group_ends = jnp.cumsum(group_sizes)
    positions = jnp.arange(number, dtype=jnp.int32)
    labels = lax.optimization_barrier(jnp.sum((group_ends[None, :] <= positions[:, None]).astype(jnp.int32), axis=1))
    return (labels[:, None] == jnp.arange(group_sizes.shape[0], dtype=jnp.int32)[None, :]).astype(jnp.float32)

def select(member, table):
    return lax.optimization_barrier(jnp.sum(member[:, :, None] * table[None], axis=1))

def reference(activations, cotangent, dw_kernel, norm_gain, norm_bias, w_in, b_in, w_out, layer_scale, group_sizes):
    images = activations.shape[0]
    row_count = IMG_H * IMG_W
    member = group_member(group_sizes, images)
    counts = group_sizes.astype(jnp.float32) * row_count
    source = activations.astype(jnp.float32)
    filtered = depthwise(source, dw_kernel).reshape(images, row_count, C)
    firsts = lax.optimization_barrier(jnp.sum(filtered, axis=1))
    seconds = lax.optimization_barrier(jnp.sum(filtered * filtered, axis=1))
    group_mean = lax.optimization_barrier(jnp.sum(member[:, :, None] * firsts[:, None, :], axis=0)) / counts[:, None]
    group_var = lax.optimization_barrier(jnp.sum(member[:, :, None] * seconds[:, None, :], axis=0)) / counts[:, None] - group_mean * group_mean
    group_rstd = lax.rsqrt(group_var + EPS)
    image_mean = select(member, group_mean)
    image_rstd = select(member, group_rstd)
    image_gain = select(member, norm_gain)
    image_bias = select(member, norm_bias)
    image_count = lax.optimization_barrier(jnp.sum(member * counts[None, :], axis=1))
    centered = (filtered - image_mean[:, None, :]) * image_rstd[:, None, :]
    normed = (centered * image_gain[:, None, :] + image_bias[:, None, :]).astype(jnp.bfloat16)
    upstream = cotangent.reshape(images, row_count, C)
    plain = source.reshape(images, row_count, C)
    block = HID // N_CHAN
    in_blocks = w_in.astype(jnp.float32).reshape(C, N_CHAN, block).transpose(1, 0, 2)
    out_blocks = w_out.astype(jnp.float32).reshape(N_CHAN, block, C)
    contract_rows = (((0,), (0,)), ((), ()))
    contract_cols = (((1,), (1,)), ((), ()))

    def step(carry, inputs):
        grad_in, grad_out, grad_bias, grad_scale = carry
        features, incoming, initial = inputs
        hidden = jnp.dot(features, w_in, preferred_element_type=jnp.float32) + b_in
        activated = jax.nn.gelu(hidden).astype(jnp.bfloat16)
        pieces = jnp.einsum('rnh,nhc->nrc', activated.astype(jnp.float32).reshape(row_count, N_CHAN, block), out_blocks, precision=lax.Precision.HIGHEST)
        rounded = lax.optimization_barrier(pieces.astype(jnp.bfloat16))
        branch = lax.optimization_barrier(jnp.sum(rounded.astype(jnp.float32), axis=0))
        incoming_f = incoming.astype(jnp.float32)
        output_rows = (initial + layer_scale * branch).astype(jnp.bfloat16)
        grad_scale = grad_scale + lax.optimization_barrier(jnp.sum(incoming_f * branch, axis=0))
        d_branch = (incoming_f * layer_scale).astype(jnp.bfloat16)
        grad_out = grad_out + lax.dot_general(activated, d_branch, contract_rows, preferred_element_type=jnp.float32)
        d_activated = lax.dot_general(d_branch, w_out, contract_cols, preferred_element_type=jnp.float32)
        _, pullback = jax.vjp(jax.nn.gelu, hidden)
        d_hidden = pullback(d_activated)[0]
        grad_bias = grad_bias + lax.optimization_barrier(jnp.sum(d_hidden, axis=0))
        hidden_b = d_hidden.astype(jnp.bfloat16)
        grad_in = grad_in + lax.dot_general(features, hidden_b, contract_rows, preferred_element_type=jnp.float32)
        backward = jnp.einsum('rnh,nch->nrc', hidden_b.astype(jnp.float32).reshape(row_count, N_CHAN, block), in_blocks, precision=lax.Precision.HIGHEST)
        d_normed = lax.optimization_barrier(jnp.sum(lax.optimization_barrier(backward.astype(jnp.bfloat16)).astype(jnp.float32), axis=0))
        return ((grad_in, grad_out, grad_bias, grad_scale), (output_rows, d_normed))
    start = (jnp.zeros((C, HID), jnp.float32), jnp.zeros((HID, C), jnp.float32), jnp.zeros((HID,), jnp.float32), jnp.zeros((C,), jnp.float32))
    finals, outputs = lax.scan(step, start, (normed, upstream, plain))
    grad_in, grad_out, grad_bias, grad_scale = finals
    output_rows, d_normed = outputs
    gain_terms = lax.optimization_barrier(jnp.sum(d_normed * centered, axis=1))
    bias_terms = lax.optimization_barrier(jnp.sum(d_normed, axis=1))
    d_gain = lax.optimization_barrier(jnp.sum(member[:, :, None] * gain_terms[:, None, :], axis=0))
    d_bias = lax.optimization_barrier(jnp.sum(member[:, :, None] * bias_terms[:, None, :], axis=0))
    image_dgain = select(member, d_gain)
    image_dbias = select(member, d_bias)
    scaled = image_gain[:, None, :] * image_rstd[:, None, :]
    d_filtered = scaled * (d_normed - image_dbias[:, None, :] / image_count[:, None, None] - centered * image_dgain[:, None, :] / image_count[:, None, None])
    d_filtered = d_filtered.reshape(images, IMG_H, IMG_W, C)
    d_kernel = kernel_grad(source, d_filtered)
    d_input = (cotangent.astype(jnp.float32) + depthwise(d_filtered, dw_kernel[::-1])).astype(jnp.bfloat16)
    result = output_rows.reshape(images, IMG_H, IMG_W, C)
    return (result, d_input, d_kernel, d_gain, d_bias, grad_in, grad_bias, grad_out, grad_scale)
```

```python
import functools

import jax
import jax.numpy as jnp
from jax import lax
from jax.experimental import pallas as pl
from jax.experimental.pallas import tpu as pltpu
from jax.sharding import PartitionSpec as P

KS = 7


EPS = 1e-05


REACH = KS // 2
SUB = 8
LANE = 128


def fill_shifts(rows, width, load_row, shifts_ref):
    def one(r, carry):
        value = load_row(r)
        column = lax.broadcasted_iota(jnp.int32, value.shape, 0)
        for c in range(KS):
            off = c - REACH
            if off == 0:
                shifts_ref[c, r] = value
            else:
                moved = pltpu.roll(value, (-off) % width, 0)
                keep = (column + off >= 0) & (column + off < width)
                shifts_ref[c, r] = jnp.where(keep, moved, 0.0)
        return carry

    lax.fori_loop(0, rows, one, 0)


def conv_forward(rows, width, channels, shifts_ref, kernel_ref, out_ref, moments_ref):
    for lb in range(channels // LANE):
        lanes = slice(lb * LANE, (lb + 1) * LANE)

        def block(sb, carry):
            first, second = carry
            cols = pl.ds(pl.multiple_of(sb * SUB, SUB), SUB)
            acc = [None] * rows
            for c in range(KS):
                taps = [kernel_ref[a * KS + c : a * KS + c + 1, lanes] for a in range(KS)]
                for r_in in range(rows):
                    value = shifts_ref[c, r_in, cols, lanes]
                    for a in range(KS):
                        r = r_in - a + REACH
                        if 0 <= r < rows:
                            term = value * taps[a]
                            acc[r] = term if acc[r] is None else acc[r] + term
            for r in range(rows):
                out_ref[r, cols, lanes] = acc[r]
                first = first + acc[r]
                second = second + acc[r] * acc[r]
            return first, second

        zero = jnp.zeros((SUB, LANE), jnp.float32)
        first, second = lax.fori_loop(0, width // SUB, block, (zero, zero))
        moments_ref[0:1, lanes] = jnp.sum(first, axis=0, keepdims=True)
        moments_ref[1:2, lanes] = jnp.sum(second, axis=0, keepdims=True)


def conv_backward(rows, width, channels, shifts_ref, source_ref, kernel_ref, grad_ref, taps_ref):
    for lb in range(channels // LANE):
        lanes = slice(lb * LANE, (lb + 1) * LANE)
        taps_ref[:, :, lanes] = jnp.zeros((KS * KS, SUB, LANE), jnp.float32)

        def block(sb, carry):
            cols = pl.ds(pl.multiple_of(sb * SUB, SUB), SUB)
            acc = [None] * rows
            xs = [source_ref[r, cols, lanes] for r in range(rows)]
            for c in range(KS):
                b = KS - 1 - c
                taps = [
                    kernel_ref[(KS - 1 - a) * KS + b : (KS - 1 - a) * KS + b + 1, lanes]
                    for a in range(KS)
                ]
                sums = [None] * KS
                for r_in in range(rows):
                    value = shifts_ref[c, r_in, cols, lanes]
                    for a in range(KS):
                        r = r_in - a + REACH
                        if 0 <= r < rows:
                            term = value * taps[a]
                            acc[r] = term if acc[r] is None else acc[r] + term
                        x_row = r_in + a - REACH
                        if 0 <= x_row < rows:
                            term = value * xs[x_row]
                            sums[a] = term if sums[a] is None else sums[a] + term
                for a in range(KS):
                    taps_ref[a * KS + b, :, lanes] += sums[a]
            for r in range(rows):
                grad_ref[r, cols, lanes] = acc[r]
            return carry

        lax.fori_loop(0, width // SUB, block, 0)


def forward_kernel(x_ref, kernel_ref, out_ref, moments_ref, shifts_ref):
    _, rows, width, channels = x_ref.shape
    fill_shifts(rows, width, lambda r: x_ref[0, r].astype(jnp.float32), shifts_ref)
    conv_forward(rows, width, channels, shifts_ref, kernel_ref, out_ref, moments_ref)


def backward_kernel(
    x_ref, cot_ref, kernel_ref, dn_ref, filt_ref, stat_ref, din_ref, dk_ref,
    shifts_ref, source_ref, grad_ref, taps_ref
):
    _, rows, width, channels = x_ref.shape

    def convert(r, carry):
        source_ref[r] = x_ref[0, r].astype(jnp.float32)
        return carry

    lax.fori_loop(0, rows, convert, 0)
    mean, rstd, scale = stat_ref[0:1], stat_ref[1:2], stat_ref[2:3]
    mean_bias, mean_gain = stat_ref[3:4], stat_ref[4:5]

    def load_row(r):
        centered = (filt_ref[r] - mean) * rstd
        return scale * (dn_ref[r].astype(jnp.float32) - mean_bias - centered * mean_gain)

    fill_shifts(rows, width, load_row, shifts_ref)
    conv_backward(
        rows, width, channels, shifts_ref, source_ref, kernel_ref, grad_ref, taps_ref
    )
    for tap in range(KS * KS):
        dk_ref[tap : tap + 1] = jnp.sum(taps_ref[tap], axis=0, keepdims=True)

    def finish(r, carry):
        din_ref[0, r] = (cot_ref[0, r].astype(jnp.float32) + grad_ref[r]).astype(jnp.bfloat16)
        return carry

    lax.fori_loop(0, rows, finish, 0)


VMEM = pl.BlockSpec(memory_space=pltpu.VMEM)
PARAMS = pltpu.CompilerParams(vmem_limit_bytes=50 * 1024 * 1024)


def group_owners(group_sizes, number):
    group_ends = jnp.cumsum(group_sizes)
    positions = jnp.arange(number, dtype=jnp.int32)
    labels = jnp.sum((group_ends[None, :] <= positions[:, None]).astype(jnp.int32), axis=1)
    return (jnp.arange(group_sizes.shape[0], dtype=jnp.int32)[:, None] == labels[None, :]).astype(
        jnp.float32
    )


def body(
    activations,
    cotangent,
    dw_kernel,
    norm_gain,
    norm_bias,
    w_in,
    b_in,
    w_out,
    layer_scale,
    group_sizes,
):
    height, width, channels = (activations.shape[1], activations.shape[2], activations.shape[3])
    row_count = height * width
    devices = lax.axis_size("dp")
    position = lax.axis_index("dp")
    group_ends = jnp.cumsum(group_sizes)
    own_group = jnp.sum((group_ends <= position).astype(jnp.int32))
    member = (jnp.arange(group_sizes.shape[0], dtype=jnp.int32) == own_group).astype(jnp.float32)
    counts = group_sizes.astype(jnp.float32) * row_count
    own_count = jnp.sum(member * counts)
    source = activations.astype(jnp.float32)
    filtered_image, moments = pl.pallas_call(
        forward_kernel,
        out_shape=(
            jax.ShapeDtypeStruct((height, width, channels), jnp.float32),
            jax.ShapeDtypeStruct((2, channels), jnp.float32),
        ),
        in_specs=[VMEM] * 2,
        out_specs=(VMEM, VMEM),
        scratch_shapes=[pltpu.VMEM((KS, height, width, channels), jnp.float32)],
        compiler_params=PARAMS,
    )(activations, dw_kernel)
    filtered = filtered_image.reshape(row_count, channels)
    per_device = lax.all_gather(moments[None], "dp", axis=0, tiled=True)
    owners = group_owners(group_sizes, devices)
    totals = jnp.sum(owners[:, :, None, None] * per_device[None], axis=1)
    group_mean = totals[:, 0] / counts[:, None]
    group_var = totals[:, 1] / counts[:, None] - group_mean * group_mean
    group_rstd = lax.rsqrt(group_var + EPS)
    own_mean = jnp.sum(member[:, None] * group_mean, axis=0)
    own_rstd = jnp.sum(member[:, None] * group_rstd, axis=0)
    own_gain = jnp.sum(member[:, None] * norm_gain, axis=0)
    own_bias = jnp.sum(member[:, None] * norm_bias, axis=0)
    centered = (filtered - own_mean) * own_rstd
    normed = (centered * own_gain + own_bias).astype(jnp.bfloat16)
    gathered = lax.all_gather(normed, "chan", axis=1, tiled=True)
    hidden = jnp.dot(gathered, w_in, preferred_element_type=jnp.float32) + b_in
    activated = jax.nn.gelu(hidden).astype(jnp.bfloat16)
    partial_branch = jnp.dot(activated, w_out, preferred_element_type=jnp.float32)
    branch = lax.psum_scatter(
        partial_branch.astype(jnp.bfloat16), "chan", scatter_dimension=1, tiled=True
    ).astype(jnp.float32)
    initial = source.reshape(row_count, channels)
    result = (initial + layer_scale * branch).astype(jnp.bfloat16).reshape(activations.shape)
    incoming = cotangent.reshape(row_count, channels).astype(jnp.float32)
    scale_local = jnp.sum(incoming * branch, axis=0)
    d_branch = (incoming * layer_scale).astype(jnp.bfloat16)
    branch_full = lax.all_gather(d_branch, "chan", axis=1, tiled=True)
    contract_rows = (((0,), (0,)), ((), ()))
    contract_cols = (((1,), (1,)), ((), ()))
    out_local_t = lax.dot_general(
        branch_full, activated, contract_rows, preferred_element_type=jnp.float32
    )
    d_activated = lax.dot_general(
        branch_full, w_out, contract_cols, preferred_element_type=jnp.float32
    )
    _, pullback = jax.vjp(jax.nn.gelu, hidden)
    d_hidden = pullback(d_activated)[0]
    bias_local = jnp.sum(d_hidden, axis=0)
    hidden_b = d_hidden.astype(jnp.bfloat16)
    in_local = lax.dot_general(
        gathered, hidden_b, contract_rows, preferred_element_type=jnp.float32
    )
    hidden_cols = in_local.shape[1]
    both_local = jnp.concatenate([in_local, out_local_t], axis=1)
    both_sums = lax.psum_scatter(
        both_local.astype(jnp.bfloat16), "dp", scatter_dimension=0, tiled=True
    ).astype(jnp.float32)
    d_w_in = both_sums[:, :hidden_cols]
    d_w_out = both_sums[:, hidden_cols:].T
    partial_normed = lax.dot_general(
        hidden_b, w_in, contract_cols, preferred_element_type=jnp.float32
    )
    d_normed = lax.psum_scatter(
        partial_normed.astype(jnp.bfloat16), "chan", scatter_dimension=1, tiled=True
    ).astype(jnp.float32)
    grad_moments = jnp.stack([jnp.sum(d_normed * centered, axis=0), jnp.sum(d_normed, axis=0)])
    grad_rows = lax.all_gather(grad_moments[None], "dp", axis=0, tiled=True)
    grad_owners = group_owners(group_sizes, devices)
    grad_totals = jnp.sum(grad_owners[:, :, None, None] * grad_rows[None], axis=1)
    d_gain = grad_totals[:, 0]
    d_bias = grad_totals[:, 1]
    own_dgain = jnp.sum(member[:, None] * d_gain, axis=0)
    own_dbias = jnp.sum(member[:, None] * d_bias, axis=0)
    stats = jnp.stack(
        [own_mean, own_rstd, own_gain * own_rstd, own_dbias / own_count, own_dgain / own_count]
    )
    d_input, kernel_local = pl.pallas_call(
        backward_kernel,
        out_shape=(
            jax.ShapeDtypeStruct(activations.shape, jnp.bfloat16),
            jax.ShapeDtypeStruct((KS * KS, channels), jnp.float32),
        ),
        in_specs=[VMEM] * 6,
        out_specs=(VMEM, VMEM),
        scratch_shapes=[
            pltpu.VMEM((KS, height, width, channels), jnp.float32),
            pltpu.VMEM((height, width, channels), jnp.float32),
            pltpu.VMEM((height, width, channels), jnp.float32),
            pltpu.VMEM((KS * KS, SUB, channels), jnp.float32),
        ],
        compiler_params=PARAMS,
    )(
        activations,
        cotangent,
        dw_kernel,
        d_normed.reshape(height, width, channels),
        filtered_image,
        stats,
    )
    d_kernel, d_b_in, d_scale = lax.psum((kernel_local, bias_local, scale_local), "dp")
    return (result, d_input, d_kernel, d_gain, d_bias, d_w_in, d_b_in, d_w_out, d_scale)


def solution(mesh):
    in_specs = (
        P("dp", None, None, "chan"),
        P("dp", None, None, "chan"),
        P(None, "chan"),
        P(None, "chan"),
        P(None, "chan"),
        P(None, "chan"),
        P("chan"),
        P("chan", None),
        P("chan"),
        P(),
    )
    out_specs = (
        P("dp", None, None, "chan"),
        P("dp", None, None, "chan"),
        P(None, "chan"),
        P(None, "chan"),
        P(None, "chan"),
        P("dp", "chan"),
        P("chan"),
        P("chan", "dp"),
        P("chan"),
    )
    return jax.shard_map(body, mesh=mesh, in_specs=in_specs, out_specs=out_specs, check_vma=False)
```

```python
import functools

import jax
import jax.numpy as jnp
from jax import lax
from jax.experimental import pallas as pl
from jax.experimental.pallas import tpu as pltpu
from jax.sharding import PartitionSpec as P

KS = 7


EPS = 1e-05


REACH = KS // 2
SUB = 8
LANE = 128


def fill_shifts(rows, width, load_row, shifts_ref):
    def one(r, carry):
        value = load_row(r)
        column = lax.broadcasted_iota(jnp.int32, value.shape, 0)
        for c in range(KS):
            off = c - REACH
            if off == 0:
                shifts_ref[c, r] = value
            else:
                moved = pltpu.roll(value, (-off) % width, 0)
                keep = (column + off >= 0) & (column + off < width)
                shifts_ref[c, r] = jnp.where(keep, moved, 0.0)
        return carry

    lax.fori_loop(0, rows, one, 0)


def conv_forward(rows, width, channels, shifts_ref, kernel_ref, out_ref, moments_ref):
    for lb in range(channels // LANE):
        lanes = slice(lb * LANE, (lb + 1) * LANE)

        def block(sb, carry):
            first, second = carry
            cols = pl.ds(pl.multiple_of(sb * SUB, SUB), SUB)
            acc = [None] * rows
            for c in range(KS):
                taps = [kernel_ref[a * KS + c : a * KS + c + 1, lanes] for a in range(KS)]
                for r_in in range(rows):
                    value = shifts_ref[c, r_in, cols, lanes]
                    for a in range(KS):
                        r = r_in - a + REACH
                        if 0 <= r < rows:
                            term = value * taps[a]
                            acc[r] = term if acc[r] is None else acc[r] + term
            for r in range(rows):
                out_ref[r, cols, lanes] = acc[r]
                first = first + acc[r]
                second = second + acc[r] * acc[r]
            return first, second

        zero = jnp.zeros((SUB, LANE), jnp.float32)
        first, second = lax.fori_loop(0, width // SUB, block, (zero, zero))
        moments_ref[0:1, lanes] = jnp.sum(first, axis=0, keepdims=True)
        moments_ref[1:2, lanes] = jnp.sum(second, axis=0, keepdims=True)


def conv_backward(rows, width, channels, shifts_ref, source_ref, kernel_ref, grad_ref, taps_ref):
    for lb in range(channels // LANE):
        lanes = slice(lb * LANE, (lb + 1) * LANE)
        taps_ref[:, :, lanes] = jnp.zeros((KS * KS, SUB, LANE), jnp.float32)

        def block(sb, carry):
            cols = pl.ds(pl.multiple_of(sb * SUB, SUB), SUB)
            acc = [None] * rows
            xs = [source_ref[r, cols, lanes] for r in range(rows)]
            for c in range(KS):
                b = KS - 1 - c
                taps = [
                    kernel_ref[(KS - 1 - a) * KS + b : (KS - 1 - a) * KS + b + 1, lanes]
                    for a in range(KS)
                ]
                sums = [None] * KS
                for r_in in range(rows):
                    value = shifts_ref[c, r_in, cols, lanes]
                    for a in range(KS):
                        r = r_in - a + REACH
                        if 0 <= r < rows:
                            term = value * taps[a]
                            acc[r] = term if acc[r] is None else acc[r] + term
                        x_row = r_in + a - REACH
                        if 0 <= x_row < rows:
                            term = value * xs[x_row]
                            sums[a] = term if sums[a] is None else sums[a] + term
                for a in range(KS):
                    taps_ref[a * KS + b, :, lanes] += sums[a]
            for r in range(rows):
                grad_ref[r, cols, lanes] = acc[r]
            return carry

        lax.fori_loop(0, width // SUB, block, 0)


MESH = pl.DeviceIdType.MESH
F32 = jnp.float32
BF16 = jnp.bfloat16
CONTRACT_ROWS = (((0,), (0,)), ((), ()))
CONTRACT_COLS = (((1,), (1,)), ((), ()))
GELU_SCALE = 0.7978845608028654
GELU_CUBE = 0.044715


def gelu_and_slope(h):
    square = h * h
    t = jnp.tanh(GELU_SCALE * (h + GELU_CUBE * (square * h)))
    half = 0.5 * (1.0 + t)
    slope = half + (0.5 * h) * (1.0 - t * t) * (
        GELU_SCALE * (1.0 + (3.0 * GELU_CUBE) * square)
    )
    return h * half, slope


def block_kernel(
    n_dp, n_y, n_chan, chunks,
    sizes_ref, x_hbm, cot_hbm, taps_in, gain_ref, bias_ref, w_in_hbm, b_in_ref, w_out_hbm, scale_ref,
    result_ref, din_ref, dk_ref, dgain_ref, dbias_ref, dwin_ref, dbin_ref, dwout_ref, dscale_ref,
    x_ref, cot_ref, w_in, w_out, source, filt, shifts, tap_sums,
    gath, dfull, d_act, act, hid_b,
    sib_send, sib_recv, own_part, x_send, x_recv, dn,
    mom_send, mom_recv, w_send, w_recv, z_send, z_recv,
    pack_y, pack_z, bias_acc,
    in_sems, ag_xs, ag_xr, ag_ss, ag_sr, ag_fs, ag_fr,
    rs_ss, rs_sr, rs_xs, rs_xr, mom_ss, mom_sr, wy_s, wy_r, wz_s, wz_r, py_s, py_r, pz_s, pz_r,
):
    images, height, width, channels = x_ref.shape
    rows = height * width
    groups = gain_ref.shape[0]
    hid = b_in_ref.shape[1]
    n_z = n_dp // n_y
    n_x = n_chan // 2
    step = rows // chunks
    step_h = height // chunks
    me_dp = lax.axis_index("dp")
    me_z, me_y = lax.div(me_dp, n_y), lax.rem(me_dp, n_y)
    me_c = lax.axis_index("chan")
    me_x, core = lax.div(me_c, 2), lax.rem(me_c, 2)
    sib = me_x * 2 + (1 - core)
    sends = []

    def other(me, n, o):
        return lax.rem(me + o, n)

    def remote(src, dst, ss, rs, **device):
        return pltpu.make_async_remote_copy(
            src_ref=src, dst_ref=dst, send_sem=ss, recv_sem=rs,
            device_id=device, device_id_type=MESH,
        )

    def send(*args, **device):
        copy = remote(*args, **device)
        copy.start()
        sends.append(copy)

    loads = [
        pltpu.make_async_copy(a, b, in_sems.at[n])
        for n, (a, b) in enumerate(
            ((cot_hbm, cot_ref), (x_hbm, x_ref), (w_out_hbm, w_out), (w_in_hbm, w_in))
        )
    ]
    for load in loads:
        load.start()

    barrier = pltpu.get_barrier_semaphore()
    for o in range(1, n_chan):
        pl.semaphore_signal(
            barrier, inc=1, device_id={"chan": other(me_c, n_chan, o)}, device_id_type=MESH
        )
    for o in range(1, n_dp):
        pl.semaphore_signal(
            barrier, inc=1, device_id={"dp": other(me_dp, n_dp, o)}, device_id_type=MESH
        )
    pl.semaphore_wait(barrier, n_chan + n_dp - 2)

    def gather_start(buf, j, lo, size):
        part = buf.at[me_c, pl.ds(lo, size)]
        for o in range(1, n_x):
            q = other(me_x, n_x, o)
            send(part, part, ag_xs.at[o, j], ag_xr.at[me_x, j], chan=q * 2 + core)
        send(part, part, ag_ss.at[j], ag_sr.at[j], chan=sib)

    def gather_relay(buf, j, lo, size):
        for o in range(1, n_x):
            q = other(me_x, n_x, o)
            part = buf.at[q * 2 + core, pl.ds(lo, size)]
            remote(part, part, ag_xs.at[o, j], ag_xr.at[q, j], chan=q * 2 + core).wait_recv()
            send(part, part, ag_fs.at[o, j], ag_fr.at[q, j], chan=sib)

    def gather_wait(buf, j, lo, size):
        part = buf.at[sib, pl.ds(lo, size)]
        remote(part, part, ag_ss.at[j], ag_sr.at[j], chan=sib).wait_recv()
        for o in range(1, n_x):
            q = other(me_x, n_x, o)
            part = buf.at[q * 2 + 1 - core, pl.ds(lo, size)]
            remote(part, part, ag_fs.at[o, j], ag_fr.at[q, j], chan=sib).wait_recv()

    def moments_send(turn):
        for o in range(1, n_dp):
            d = other(me_dp, n_dp, o)
            send(
                mom_send.at[turn], mom_recv.at[turn, me_dp],
                mom_ss.at[turn, o], mom_sr.at[turn, me_dp], dp=d,
            )

    def moments_wait(turn):
        for o in range(1, n_dp):
            d = other(me_dp, n_dp, o)
            remote(
                mom_send.at[turn], mom_recv.at[turn, d],
                mom_ss.at[turn, o], mom_sr.at[turn, d], dp=d,
            ).wait_recv()

    def label_of(d):
        end = jnp.int32(0)
        label = jnp.int32(0)
        for g in range(groups):
            end = end + sizes_ref[g]
            label = label + (end <= d).astype(jnp.int32)
        return label

    mine = label_of(me_dp)
    count = jnp.float32(0)
    own_gain = jnp.zeros((1, channels), F32)
    own_bias = jnp.zeros((1, channels), F32)
    for g in range(groups):
        is_mine = (mine == g).astype(F32)
        count = count + is_mine * (sizes_ref[g] * rows).astype(F32)
        own_gain = own_gain + is_mine * gain_ref[g : g + 1]
        own_bias = own_bias + is_mine * bias_ref[g : g + 1]
    count = jnp.full((1, channels), count, F32)

    loads[0].wait()
    for i in range(chunks):
        lo = i * step
        cot = cot_ref[0, i * step_h : (i + 1) * step_h].reshape(step, channels)
        dfull[me_c, lo : lo + step] = (cot.astype(F32) * scale_ref[...]).astype(BF16)
    gather_start(dfull, chunks, 0, rows)

    loads[1].wait()

    def load_x(r):
        value = x_ref[0, r].astype(F32)
        source[r] = value
        return value

    fill_shifts(height, width, load_x, shifts)
    mom_send[0] = jnp.zeros(mom_send.shape[1:], F32)
    conv_forward(height, width, channels, shifts, taps_in, filt, mom_send.at[0])
    moments_send(0)
    gather_relay(dfull, chunks, 0, rows)
    loads[2].wait()
    moments_wait(0)
    mom_recv[0, me_dp] = mom_send[0]
    total = jnp.zeros(mom_send.shape[1:], F32)
    for d in range(n_dp):
        total = total + (label_of(d) == mine).astype(F32) * mom_recv[0, d]
    mean = total[0:1] / count
    rstd = lax.rsqrt(total[1:2] / count - mean * mean + EPS)

    for i in range(chunks):
        lo = i * step
        part = filt[i * step_h : (i + 1) * step_h].reshape(step, channels)
        centered = (part - mean) * rstd
        gath[me_c, lo : lo + step] = (centered * own_gain + own_bias).astype(BF16)
        gather_start(gath, i, lo, step)

    gather_wait(dfull, chunks, 0, rows)
    loads[3].wait()
    tile = 256

    def d_act_tile(n, carry):
        lo = pl.multiple_of(n * tile, tile)
        value = jnp.zeros((tile, hid), F32)
        for k in range(n_chan):
            value = value + lax.dot_general(
                dfull[k, pl.ds(lo, tile)], w_out[:, k * channels : (k + 1) * channels],
                CONTRACT_COLS, preferred_element_type=F32,
            )
        d_act[pl.ds(lo, tile)] = value
        return carry

    lax.fori_loop(0, rows // tile, d_act_tile, 0)
    bias_acc[...] = jnp.zeros(bias_acc.shape, F32)

    def hidden_chunk(lo):
        def one(n, carry):
            cols = pl.ds(pl.multiple_of(n * tile, tile), tile)
            value = jnp.zeros((step, tile), F32)
            for k in range(n_chan):
                value = value + jnp.dot(
                    gath[k, lo : lo + step], w_in[k * channels : (k + 1) * channels, cols],
                    preferred_element_type=F32,
                )
            value = value + b_in_ref[:, cols]
            out, slope = gelu_and_slope(value)
            act[lo : lo + step, cols] = out.astype(BF16)
            d_hid = d_act[lo : lo + step, cols] * slope
            bias_acc[0:1, cols] += jnp.sum(d_hid, axis=0, keepdims=True)
            hid_b[lo : lo + step, cols] = d_hid.astype(BF16)
            return carry

        lax.fori_loop(0, hid // tile, one, 0)

    def scatter_sibling(kind, i, product):
        lo = i * step
        for q in range(n_x):
            value = product(lo, q * 2 + 1 - core)
            sib_send[kind, i, q] = value.astype(BF16)
        send(
            sib_send.at[kind, i], sib_recv.at[kind, i],
            rs_ss.at[kind, i], rs_sr.at[kind, i], chan=sib,
        )
        for q in range(n_x):
            own_part[kind, q, lo : lo + step] = product(lo, q * 2 + core).astype(BF16)

    def scatter_chips(kind, i):
        lo = i * step
        remote(
            sib_send.at[kind, i], sib_recv.at[kind, i],
            rs_ss.at[kind, i], rs_sr.at[kind, i], chan=sib,
        ).wait_recv()
        for o in range(1, n_x):
            q = other(me_x, n_x, o)
            both = own_part[kind, q, lo : lo + step].astype(F32) + sib_recv[kind, i, q].astype(F32)
            x_send[kind, o, lo : lo + step] = both.astype(BF16)
            send(
                x_send.at[kind, o, pl.ds(lo, step)], x_recv.at[kind, me_x, pl.ds(lo, step)],
                rs_xs.at[kind, o, i], rs_xr.at[kind, me_x, i], chan=q * 2 + core,
            )

    def scatter_finish(kind, i):
        lo = i * step
        value = own_part[kind, me_x, lo : lo + step].astype(F32)
        value = value + sib_recv[kind, i, me_x].astype(F32)
        for o in range(1, n_x):
            q = other(me_x, n_x, o)
            remote(
                x_send.at[kind, o, pl.ds(lo, step)], x_recv.at[kind, q, pl.ds(lo, step)],
                rs_xs.at[kind, o, i], rs_xr.at[kind, q, i], chan=q * 2 + core,
            ).wait_recv()
            value = value + x_recv[kind, q, lo : lo + step].astype(F32)
        return value

    def normed_product(lo, k):
        weight = w_in[pl.ds(pl.multiple_of(k * channels, channels), channels), :]
        return lax.dot_general(
            hid_b[lo : lo + step], weight, CONTRACT_COLS, preferred_element_type=F32
        )

    def branch_product(lo, k):
        weight = w_out[:, pl.ds(pl.multiple_of(k * channels, channels), channels)]
        return jnp.dot(act[lo : lo + step], weight, preferred_element_type=F32)

    gather_relay(gath, 0, 0, step)
    for i in range(chunks):
        if i + 1 < chunks:
            gather_relay(gath, i + 1, (i + 1) * step, step)
        gather_wait(gath, i, i * step, step)
        hidden_chunk(i * step)
        scatter_sibling(0, i, normed_product)
        if i >= 1:
            scatter_chips(0, i - 1)
    scatter_chips(0, chunks - 1)

    part_rows = w_send.shape[2]
    per = channels // part_rows

    def weight_grad(t, left, right):
        for k in range(n_chan):
            value = lax.dot_general(
                left[k], right[...], CONTRACT_ROWS, preferred_element_type=F32
            ).astype(BF16)
            for j in range(per):
                d = k * per + j
                w_send[t, (d % n_y) * n_z + d // n_y] = value[j * part_rows : (j + 1) * part_rows]
        for o in range(1, n_y):
            y = other(me_y, n_y, o)
            send(
                w_send.at[t, pl.ds(y * n_z, n_z)], w_recv.at[t, me_y],
                wy_s.at[t, o], wy_r.at[t, me_y], dp=me_z * n_y + y,
            )

    weight_grad(1, dfull, act)
    weight_grad(0, gath, hid_b)

    for i in range(chunks):
        scatter_sibling(1, i, branch_product)
        if i >= 1:
            scatter_chips(1, i - 1)
    scatter_chips(1, chunks - 1)

    gain_term = jnp.zeros((1, channels), F32)
    bias_term = jnp.zeros((1, channels), F32)
    for i in range(chunks):
        value = scatter_finish(0, i)
        part = filt[i * step_h : (i + 1) * step_h].reshape(step, channels)
        centered = (part - mean) * rstd
        gain_term = gain_term + jnp.sum(value * centered, axis=0, keepdims=True)
        bias_term = bias_term + jnp.sum(value, axis=0, keepdims=True)
        dn[i * step_h : (i + 1) * step_h] = value.reshape(step_h, width, channels)
    mom_send[1] = jnp.zeros(mom_send.shape[1:], F32)
    mom_send[1, 0:1] = gain_term
    mom_send[1, 1:2] = bias_term
    moments_send(1)
    mom_recv[1, me_dp] = mom_send[1]
    moments_wait(1)
    group_sum = [jnp.zeros(mom_send.shape[1:], F32) for _ in range(groups)]
    for d in range(n_dp):
        value = mom_recv[1, d]
        label = label_of(d)
        for g in range(groups):
            group_sum[g] = group_sum[g] + (label == g).astype(F32) * value
    own_sum = jnp.zeros(mom_send.shape[1:], F32)
    for g in range(groups):
        dgain_ref[g : g + 1] = group_sum[g][0:1]
        dbias_ref[g : g + 1] = group_sum[g][1:2]
        own_sum = own_sum + (mine == g).astype(F32) * group_sum[g]
    mean_gain, mean_bias = own_sum[0:1] / count, own_sum[1:2] / count
    factor = own_gain * rstd

    def load_row(r):
        centered = (filt[r] - mean) * rstd
        return factor * (dn[r] - mean_bias - centered * mean_gain)

    fill_shifts(height, width, load_row, shifts)
    conv_backward(height, width, channels, shifts, source, taps_in, filt, tap_sums)

    def finish_row(r, carry):
        din_ref[0, r] = (cot_ref[0, r].astype(F32) + filt[r]).astype(BF16)
        return carry

    lax.fori_loop(0, height, finish_row, 0)

    scale_sum = jnp.zeros((1, channels), F32)
    for i in range(chunks):
        branch = scatter_finish(1, i)
        cot = cot_ref[0, i * step_h : (i + 1) * step_h].reshape(step, channels).astype(F32)
        plain = source[i * step_h : (i + 1) * step_h].reshape(step, channels)
        scale_sum = scale_sum + jnp.sum(cot * branch, axis=0, keepdims=True)
        value = (plain + scale_ref[...] * branch).astype(BF16)
        result_ref[0, i * step_h : (i + 1) * step_h] = value.reshape(step_h, width, channels)

    n_taps = KS * KS
    pieces = hid // channels
    pack_y[me_y] = jnp.zeros(pack_y.shape[1:], F32)
    for tap in range(n_taps):
        pack_y[me_y, tap : tap + 1] = jnp.sum(tap_sums[tap], axis=0, keepdims=True)
    pack_y[me_y, n_taps : n_taps + 1] = scale_sum
    for p in range(pieces):
        pack_y[me_y, n_taps + 1 + p : n_taps + 2 + p] = bias_acc[
            0:1, p * channels : (p + 1) * channels
        ]
    for o in range(1, n_y):
        y = other(me_y, n_y, o)
        send(
            pack_y.at[me_y], pack_y.at[me_y], py_s.at[o], py_r.at[me_y], dp=me_z * n_y + y
        )

    def weight_stage(t):
        for o in range(1, n_y):
            y = other(me_y, n_y, o)
            remote(
                w_send.at[t, pl.ds(y * n_z, n_z)], w_recv.at[t, y],
                wy_s.at[t, o], wy_r.at[t, y], dp=me_z * n_y + y,
            ).wait_recv()
        for o in range(n_z):
            z = other(me_z, n_z, o)
            value = w_send[t, me_y * n_z + z].astype(F32)
            for p in range(1, n_y):
                value = value + w_recv[t, other(me_y, n_y, p), z].astype(F32)
            z_send[t, o] = value.astype(BF16)
            if o:
                send(
                    z_send.at[t, o], z_recv.at[t, me_z],
                    wz_s.at[t, o], wz_r.at[t, me_z], dp=z * n_y + me_y,
                )

    weight_stage(1)
    for o in range(1, n_y):
        y = other(me_y, n_y, o)
        remote(
            pack_y.at[y], pack_y.at[y], py_s.at[o], py_r.at[y], dp=me_z * n_y + y
        ).wait_recv()
    pack = pack_y[0]
    for y in range(1, n_y):
        pack = pack + pack_y[y]
    pack_z[me_z] = pack
    for o in range(1, n_z):
        z = other(me_z, n_z, o)
        send(
            pack_z.at[me_z], pack_z.at[me_z], pz_s.at[o], pz_r.at[me_z], dp=z * n_y + me_y
        )
    weight_stage(0)

    for o in range(1, n_z):
        z = other(me_z, n_z, o)
        remote(
            pack_z.at[z], pack_z.at[z], pz_s.at[o], pz_r.at[z], dp=z * n_y + me_y
        ).wait_recv()
    pack = pack_z[0]
    for z in range(1, n_z):
        pack = pack + pack_z[z]
    dk_ref[...] = pack[:n_taps]
    dscale_ref[...] = pack[n_taps : n_taps + 1]
    for p in range(pieces):
        dbin_ref[0:1, p * channels : (p + 1) * channels] = pack[n_taps + 1 + p : n_taps + 2 + p]

    def weight_finish(t):
        value = z_send[t, 0].astype(F32)
        for o in range(1, n_z):
            z = other(me_z, n_z, o)
            remote(
                z_send.at[t, o], z_recv.at[t, z], wz_s.at[t, o], wz_r.at[t, z],
                dp=z * n_y + me_y,
            ).wait_recv()
            value = value + z_recv[t, z].astype(F32)
        return value

    dwout_ref[...] = weight_finish(1).T
    dwin_ref[...] = weight_finish(0)
    for copy in sends:
        copy.wait_send()


def body(n_dp, n_chan, activations, cotangent, dw_kernel, norm_gain, norm_bias, w_in, b_in, w_out,
         layer_scale, group_sizes):
    _, height, width, channels = activations.shape
    rows = height * width
    full = w_in.shape[0]
    hid = w_in.shape[1]
    groups = norm_gain.shape[0]
    chunks = 4
    n_x = n_chan // 2
    n_y = 1
    while n_dp % (2 * n_y) == 0 and 2 * (2 * n_y) ** 2 <= n_dp:
        n_y *= 2
    n_z = n_dp // n_y
    part = full // n_dp
    step = rows // chunks
    pack_rows = -(-(KS * KS + 1 + hid // channels) // 8) * 8
    vmem = pl.BlockSpec(memory_space=pltpu.VMEM)
    hbm = pl.BlockSpec(memory_space=pl.ANY)
    smem = pl.BlockSpec(memory_space=pltpu.SMEM)
    sds = jax.ShapeDtypeStruct
    dma = pltpu.SemaphoreType.DMA
    outs = pl.pallas_call(
        functools.partial(block_kernel, n_dp, n_y, n_chan, chunks),
        out_shape=(
            sds(activations.shape, BF16),
            sds(activations.shape, BF16),
            sds((KS * KS, channels), F32),
            sds((groups, channels), F32),
            sds((groups, channels), F32),
            sds((part, hid), F32),
            sds((1, hid), F32),
            sds((hid, part), F32),
            sds((1, channels), F32),
        ),
        in_specs=[smem, hbm, hbm, vmem, vmem, vmem, hbm, vmem, hbm, vmem],
        out_specs=(vmem,) * 9,
        scratch_shapes=[
            pltpu.VMEM(activations.shape, BF16),
            pltpu.VMEM(activations.shape, BF16),
            pltpu.VMEM(w_in.shape, BF16),
            pltpu.VMEM(w_out.shape, BF16),
            pltpu.VMEM((height, width, channels), F32),
            pltpu.VMEM((height, width, channels), F32),
            pltpu.VMEM((KS, height, width, channels), F32),
            pltpu.VMEM((KS * KS, SUB, channels), F32),
            pltpu.VMEM((n_chan, rows, channels), BF16),
            pltpu.VMEM((n_chan, rows, channels), BF16),
            pltpu.VMEM((rows, hid), F32),
            pltpu.VMEM((rows, hid), BF16),
            pltpu.VMEM((rows, hid), BF16),
            pltpu.VMEM((2, chunks, n_x, step, channels), BF16),
            pltpu.VMEM((2, chunks, n_x, step, channels), BF16),
            pltpu.VMEM((2, n_x, rows, channels), BF16),
            pltpu.VMEM((2, n_x, rows, channels), BF16),
            pltpu.VMEM((2, n_x, rows, channels), BF16),
            pltpu.VMEM((height, width, channels), F32),
            pltpu.VMEM((2, 8, channels), F32),
            pltpu.VMEM((2, n_dp, 8, channels), F32),
            pltpu.VMEM((2, n_dp, part, hid), BF16),
            pltpu.VMEM((2, n_y, n_z, part, hid), BF16),
            pltpu.VMEM((2, n_z, part, hid), BF16),
            pltpu.VMEM((2, n_z, part, hid), BF16),
            pltpu.VMEM((n_y, pack_rows, channels), F32),
            pltpu.VMEM((n_z, pack_rows, channels), F32),
            pltpu.VMEM((8, hid), F32),
            dma((4,)),
            dma((n_x, chunks + 1)),
            dma((n_x, chunks + 1)),
            dma((chunks + 1,)),
            dma((chunks + 1,)),
            dma((n_x, chunks + 1)),
            dma((n_x, chunks + 1)),
            dma((2, chunks)),
            dma((2, chunks)),
            dma((2, n_x, chunks)),
            dma((2, n_x, chunks)),
            dma((2, n_dp)),
            dma((2, n_dp)),
            dma((2, n_y)),
            dma((2, n_y)),
            dma((2, n_z)),
            dma((2, n_z)),
            dma((n_y,)),
            dma((n_y,)),
            dma((n_z,)),
            dma((n_z,)),
        ],
        compiler_params=pltpu.CompilerParams(
            collective_id=0, has_side_effects=True, vmem_limit_bytes=60 * 1024 * 1024
        ),
    )(
        group_sizes, activations, cotangent, dw_kernel, norm_gain, norm_bias, w_in,
        b_in[None], w_out, layer_scale[None],
    )
    result, d_input, d_kernel, d_gain, d_bias, d_w_in, d_b_in, d_w_out, d_scale = outs
    return (result, d_input, d_kernel, d_gain, d_bias, d_w_in, d_b_in[0], d_w_out, d_scale[0])


def solution(mesh):
    step = functools.partial(body, mesh.shape["dp"], mesh.shape["chan"])
    in_specs = (
        P("dp", None, None, "chan"),
        P("dp", None, None, "chan"),
        P(None, "chan"),
        P(None, "chan"),
        P(None, "chan"),
        P(None, "chan"),
        P("chan"),
        P("chan", None),
        P("chan"),
        P(),
    )
    out_specs = (
        P("dp", None, None, "chan"),
        P("dp", None, None, "chan"),
        P(None, "chan"),
        P(None, "chan"),
        P(None, "chan"),
        P("dp", "chan"),
        P("chan"),
        P("chan", "dp"),
        P("chan"),
    )
    return jax.shard_map(step, mesh=mesh, in_specs=in_specs, out_specs=out_specs, check_vma=False)
```

```python
import functools

import jax
import jax.numpy as jnp
from jax import lax
from jax.experimental import pallas as pl
from jax.experimental.pallas import tpu as pltpu
from jax.sharding import PartitionSpec as P

KS = 7


EPS = 1e-05


REACH = KS // 2
SUB = 8
LANE = 128


def fill_shifts(rows, width, load_row, shifts_ref):
    def one(r, carry):
        value = load_row(r)
        column = lax.broadcasted_iota(jnp.int32, value.shape, 0)
        for c in range(KS):
            off = c - REACH
            if off == 0:
                shifts_ref[c, r] = value
            else:
                moved = pltpu.roll(value, (-off) % width, 0)
                keep = (column + off >= 0) & (column + off < width)
                shifts_ref[c, r] = jnp.where(keep, moved, 0.0)
        return carry

    lax.fori_loop(0, rows, one, 0)


def conv_forward(rows, width, channels, shifts_ref, kernel_ref, out_ref, moments_ref):
    for lb in range(channels // LANE):
        lanes = slice(lb * LANE, (lb + 1) * LANE)

        def block(sb, carry):
            first, second = carry
            cols = pl.ds(pl.multiple_of(sb * SUB, SUB), SUB)
            acc = [None] * rows
            for c in range(KS):
                taps = [kernel_ref[a * KS + c : a * KS + c + 1, lanes] for a in range(KS)]
                for r_in in range(rows):
                    value = shifts_ref[c, r_in, cols, lanes]
                    for a in range(KS):
                        r = r_in - a + REACH
                        if 0 <= r < rows:
                            term = value * taps[a]
                            acc[r] = term if acc[r] is None else acc[r] + term
            for r in range(rows):
                out_ref[r, cols, lanes] = acc[r]
                first = first + acc[r]
                second = second + acc[r] * acc[r]
            return first, second

        zero = jnp.zeros((SUB, LANE), jnp.float32)
        first, second = lax.fori_loop(0, width // SUB, block, (zero, zero))
        moments_ref[0:1, lanes] = jnp.sum(first, axis=0, keepdims=True)
        moments_ref[1:2, lanes] = jnp.sum(second, axis=0, keepdims=True)


def conv_backward(
    lane_blocks, rows, width, shifts_ref, source_ref, kernel_ref, grad_ref, taps_ref
):
    for lb in lane_blocks:
        lanes = slice(lb * LANE, (lb + 1) * LANE)
        taps_ref[:, :, lanes] = jnp.zeros((KS * KS, SUB, LANE), jnp.float32)

        def block(sb, carry):
            cols = pl.ds(pl.multiple_of(sb * SUB, SUB), SUB)
            acc = [None] * rows
            xs = [source_ref[r, cols, lanes] for r in range(rows)]
            for c in range(KS):
                b = KS - 1 - c
                taps = [
                    kernel_ref[(KS - 1 - a) * KS + b : (KS - 1 - a) * KS + b + 1, lanes]
                    for a in range(KS)
                ]
                sums = [None] * KS
                for r_in in range(rows):
                    value = shifts_ref[c, r_in, cols, lanes]
                    for a in range(KS):
                        r = r_in - a + REACH
                        if 0 <= r < rows:
                            term = value * taps[a]
                            acc[r] = term if acc[r] is None else acc[r] + term
                        x_row = r_in + a - REACH
                        if 0 <= x_row < rows:
                            term = value * xs[x_row]
                            sums[a] = term if sums[a] is None else sums[a] + term
                for a in range(KS):
                    taps_ref[a * KS + b, :, lanes] += sums[a]
            for r in range(rows):
                grad_ref[r, cols, lanes] = acc[r]
            return carry

        lax.fori_loop(0, width // SUB, block, 0)


MESH = pl.DeviceIdType.MESH
F32 = jnp.float32
BF16 = jnp.bfloat16
CONTRACT_ROWS = (((0,), (0,)), ((), ()))
CONTRACT_COLS = (((1,), (1,)), ((), ()))
GELU_SCALE = 0.7978845608028654
GELU_CUBE = 0.044715


def gelu_and_slope(h):
    square = h * h
    t = jnp.tanh(GELU_SCALE * (h + GELU_CUBE * (square * h)))
    half = 0.5 * (1.0 + t)
    slope = half + (0.5 * h) * (1.0 - t * t) * (
        GELU_SCALE * (1.0 + (3.0 * GELU_CUBE) * square)
    )
    return h * half, slope


def block_kernel(
    n_dp, n_y, n_chan, chunks,
    sizes_ref, x_hbm, cot_hbm, taps_in, gain_ref, bias_ref, w_in_hbm, b_in_ref, w_out_hbm, scale_ref,
    result_ref, din_ref, dk_ref, dgain_ref, dbias_ref, dwin_ref, dbin_ref, dwout_ref, dscale_ref,
    x_ref, cot_ref, w_in, w_out, source, filt, shifts, tap_sums,
    gath, dfull, d_act, act, hid_b,
    sib_send, sib_recv, own_part, x_send, x_recv, dn,
    mom_send, mom_recv, w_send, w_recv, z_send, z_recv,
    pack_y, pack_z, bias_acc,
    in_sems, ag_xs, ag_xr, ag_ss, ag_sr, ag_fs, ag_fr,
    rs_ss, rs_sr, rs_xs, rs_xr, mom_ss, mom_sr, wy_s, wy_r, wz_s, wz_r, py_s, py_r, pz_s, pz_r,
):
    images, height, width, channels = x_ref.shape
    rows = height * width
    groups = gain_ref.shape[0]
    hid = b_in_ref.shape[1]
    n_z = n_dp // n_y
    n_x = n_chan // 2
    step = rows // chunks
    step_h = height // chunks
    me_dp = lax.axis_index("dp")
    me_z, me_y = lax.div(me_dp, n_y), lax.rem(me_dp, n_y)
    me_c = lax.axis_index("chan")
    me_x, core = lax.div(me_c, 2), lax.rem(me_c, 2)
    sib = me_x * 2 + (1 - core)
    sends = []

    def other(me, n, o):
        return lax.rem(me + o, n)

    def remote(src, dst, ss, rs, **device):
        return pltpu.make_async_remote_copy(
            src_ref=src, dst_ref=dst, send_sem=ss, recv_sem=rs,
            device_id=device, device_id_type=MESH,
        )

    def send(*args, **device):
        copy = remote(*args, **device)
        copy.start()
        sends.append(copy)

    loads = [
        pltpu.make_async_copy(a, b, in_sems.at[n])
        for n, (a, b) in enumerate(
            ((cot_hbm, cot_ref), (x_hbm, x_ref), (w_out_hbm, w_out), (w_in_hbm, w_in))
        )
    ]
    for load in loads:
        load.start()

    barrier = pltpu.get_barrier_semaphore()
    for o in range(1, n_chan):
        pl.semaphore_signal(
            barrier, inc=1, device_id={"chan": other(me_c, n_chan, o)}, device_id_type=MESH
        )
    for o in range(1, n_dp):
        pl.semaphore_signal(
            barrier, inc=1, device_id={"dp": other(me_dp, n_dp, o)}, device_id_type=MESH
        )
    pl.semaphore_wait(barrier, n_chan + n_dp - 2)

    def gather_start(buf, j, lo, size):
        part = buf.at[me_c, pl.ds(lo, size)]
        for o in range(1, n_x):
            q = other(me_x, n_x, o)
            send(part, part, ag_xs.at[o, j], ag_xr.at[me_x, j], chan=q * 2 + core)
        send(part, part, ag_ss.at[j], ag_sr.at[j], chan=sib)

    def gather_relay(buf, j, lo, size):
        for o in range(1, n_x):
            q = other(me_x, n_x, o)
            part = buf.at[q * 2 + core, pl.ds(lo, size)]
            remote(part, part, ag_xs.at[o, j], ag_xr.at[q, j], chan=q * 2 + core).wait_recv()
            send(part, part, ag_fs.at[o, j], ag_fr.at[q, j], chan=sib)

    def gather_wait(buf, j, lo, size):
        part = buf.at[sib, pl.ds(lo, size)]
        remote(part, part, ag_ss.at[j], ag_sr.at[j], chan=sib).wait_recv()
        for o in range(1, n_x):
            q = other(me_x, n_x, o)
            part = buf.at[q * 2 + 1 - core, pl.ds(lo, size)]
            remote(part, part, ag_fs.at[o, j], ag_fr.at[q, j], chan=sib).wait_recv()

    def moments_send(turn):
        for o in range(1, n_dp):
            d = other(me_dp, n_dp, o)
            send(
                mom_send.at[turn], mom_recv.at[turn, me_dp],
                mom_ss.at[turn, o], mom_sr.at[turn, me_dp], dp=d,
            )

    def moments_wait(turn):
        for o in range(1, n_dp):
            d = other(me_dp, n_dp, o)
            remote(
                mom_send.at[turn], mom_recv.at[turn, d],
                mom_ss.at[turn, o], mom_sr.at[turn, d], dp=d,
            ).wait_recv()

    def label_of(d):
        end = jnp.int32(0)
        label = jnp.int32(0)
        for g in range(groups):
            end = end + sizes_ref[g]
            label = label + (end <= d).astype(jnp.int32)
        return label

    mine = label_of(me_dp)
    count = jnp.float32(0)
    own_gain = jnp.zeros((1, channels), F32)
    own_bias = jnp.zeros((1, channels), F32)
    for g in range(groups):
        is_mine = (mine == g).astype(F32)
        count = count + is_mine * (sizes_ref[g] * rows).astype(F32)
        own_gain = own_gain + is_mine * gain_ref[g : g + 1]
        own_bias = own_bias + is_mine * bias_ref[g : g + 1]
    count = jnp.full((1, channels), count, F32)

    loads[0].wait()
    for i in range(chunks):
        lo = i * step
        cot = cot_ref[0, i * step_h : (i + 1) * step_h].reshape(step, channels)
        dfull[me_c, lo : lo + step] = (cot.astype(F32) * scale_ref[...]).astype(BF16)
    gather_start(dfull, chunks, 0, rows)

    loads[1].wait()

    def load_x(r):
        value = x_ref[0, r].astype(F32)
        source[r] = value
        return value

    fill_shifts(height, width, load_x, shifts)
    mom_send[0] = jnp.zeros(mom_send.shape[1:], F32)
    conv_forward(height, width, channels, shifts, taps_in, filt, mom_send.at[0])
    moments_send(0)
    gather_relay(dfull, chunks, 0, rows)
    loads[2].wait()
    gather_wait(dfull, chunks, 0, rows)
    tile = 256

    def d_act_tile(n, carry):
        lo = pl.multiple_of(n * tile, tile)
        value = jnp.zeros((tile, hid), F32)
        for k in range(n_chan):
            value = value + lax.dot_general(
                dfull[k, pl.ds(lo, tile)], w_out[:, k * channels : (k + 1) * channels],
                CONTRACT_COLS, preferred_element_type=F32,
            )
        d_act[pl.ds(lo, tile)] = value
        return carry

    early = rows // tile // 2
    lax.fori_loop(0, early, d_act_tile, 0)
    moments_wait(0)
    mom_recv[0, me_dp] = mom_send[0]
    total = jnp.zeros(mom_send.shape[1:], F32)
    for d in range(n_dp):
        total = total + (label_of(d) == mine).astype(F32) * mom_recv[0, d]
    mean = total[0:1] / count
    rstd = lax.rsqrt(total[1:2] / count - mean * mean + EPS)

    for i in range(chunks):
        lo = i * step
        part = filt[i * step_h : (i + 1) * step_h].reshape(step, channels)
        centered = (part - mean) * rstd
        gath[me_c, lo : lo + step] = (centered * own_gain + own_bias).astype(BF16)
        gather_start(gath, i, lo, step)

    lax.fori_loop(early, rows // tile, d_act_tile, 0)
    loads[3].wait()
    bias_acc[...] = jnp.zeros(bias_acc.shape, F32)

    def hidden_chunk(lo):
        def one(n, carry):
            cols = pl.ds(pl.multiple_of(n * tile, tile), tile)
            value = jnp.zeros((step, tile), F32)
            for k in range(n_chan):
                value = value + jnp.dot(
                    gath[k, lo : lo + step], w_in[k * channels : (k + 1) * channels, cols],
                    preferred_element_type=F32,
                )
            value = value + b_in_ref[:, cols]
            out, slope = gelu_and_slope(value)
            act[lo : lo + step, cols] = out.astype(BF16)
            d_hid = d_act[lo : lo + step, cols] * slope
            bias_acc[0:1, cols] += jnp.sum(d_hid, axis=0, keepdims=True)
            hid_b[lo : lo + step, cols] = d_hid.astype(BF16)
            return carry

        lax.fori_loop(0, hid // tile, one, 0)

    def scatter_sibling(kind, i, product):
        lo = i * step
        for q in range(n_x):
            value = product(lo, q * 2 + 1 - core)
            sib_send[kind, i, q] = value.astype(BF16)
        send(
            sib_send.at[kind, i], sib_recv.at[kind, i],
            rs_ss.at[kind, i], rs_sr.at[kind, i], chan=sib,
        )
        for q in range(n_x):
            own_part[kind, q, lo : lo + step] = product(lo, q * 2 + core).astype(BF16)

    def scatter_chips(kind, i):
        lo = i * step
        remote(
            sib_send.at[kind, i], sib_recv.at[kind, i],
            rs_ss.at[kind, i], rs_sr.at[kind, i], chan=sib,
        ).wait_recv()
        for o in range(1, n_x):
            q = other(me_x, n_x, o)
            both = own_part[kind, q, lo : lo + step].astype(F32) + sib_recv[kind, i, q].astype(F32)
            x_send[kind, o, lo : lo + step] = both.astype(BF16)
            send(
                x_send.at[kind, o, pl.ds(lo, step)], x_recv.at[kind, me_x, pl.ds(lo, step)],
                rs_xs.at[kind, o, i], rs_xr.at[kind, me_x, i], chan=q * 2 + core,
            )

    def scatter_finish(kind, i):
        lo = i * step
        value = own_part[kind, me_x, lo : lo + step].astype(F32)
        value = value + sib_recv[kind, i, me_x].astype(F32)
        for o in range(1, n_x):
            q = other(me_x, n_x, o)
            remote(
                x_send.at[kind, o, pl.ds(lo, step)], x_recv.at[kind, q, pl.ds(lo, step)],
                rs_xs.at[kind, o, i], rs_xr.at[kind, q, i], chan=q * 2 + core,
            ).wait_recv()
            value = value + x_recv[kind, q, lo : lo + step].astype(F32)
        return value

    def normed_product(lo, k):
        weight = w_in[pl.ds(pl.multiple_of(k * channels, channels), channels), :]
        return lax.dot_general(
            hid_b[lo : lo + step], weight, CONTRACT_COLS, preferred_element_type=F32
        )

    def branch_product(lo, k):
        weight = w_out[:, pl.ds(pl.multiple_of(k * channels, channels), channels)]
        return jnp.dot(act[lo : lo + step], weight, preferred_element_type=F32)

    gather_relay(gath, 0, 0, step)
    for i in range(chunks):
        if i + 1 < chunks:
            gather_relay(gath, i + 1, (i + 1) * step, step)
        gather_wait(gath, i, i * step, step)
        hidden_chunk(i * step)

    part_rows = w_send.shape[2]
    per = channels // part_rows

    order = [o % n_z for o in range(1, n_z + 1)]

    def weight_block(t, left, right, k):
        value = lax.dot_general(
            left[k], right[...], CONTRACT_ROWS, preferred_element_type=F32
        ).astype(BF16)
        for j in range(per):
            d = k * per + j
            slot = lax.rem(d, n_y) * n_z + lax.div(d, n_y)
            w_send[t, slot] = value[j * part_rows : (j + 1) * part_rows]

    def weight_copy(t, o, p):
        y, z = other(me_y, n_y, p), other(me_z, n_z, o)
        return (
            w_send.at[t, y * n_z + z], w_recv.at[t, me_y, z],
            wy_s.at[t, p, o], wy_r.at[t, me_y, z],
        ), me_z * n_y + y

    def weight_issue(t, o):
        for p in range(1, n_y):
            args, d = weight_copy(t, o, p)
            send(*args, dp=d)

    def weight_grad(t, left, right, issue):
        if per == n_y:
            for o in order:
                weight_block(t, left, right, other(me_z, n_z, o))
                if issue:
                    weight_issue(t, o)
        else:
            for k in range(n_chan):
                weight_block(t, left, right, jnp.int32(k))
            if issue:
                for o in order:
                    weight_issue(t, o)

    def weight_stage(t, o):
        z = other(me_z, n_z, o)
        value = w_send[t, me_y * n_z + z].astype(F32)
        for p in range(1, n_y):
            y = other(me_y, n_y, p)
            remote(
                w_send.at[t, y * n_z + z], w_recv.at[t, y, z],
                wy_s.at[t, p, o], wy_r.at[t, y, z], dp=me_z * n_y + y,
            ).wait_recv()
            value = value + w_recv[t, y, z].astype(F32)
        z_send[t, o] = value.astype(BF16)
        if o:
            send(
                z_send.at[t, o], z_recv.at[t, me_z],
                wz_s.at[t, o], wz_r.at[t, me_z], dp=z * n_y + me_y,
            )

    weight_grad(1, dfull, act, True)
    for i in range(chunks):
        scatter_sibling(0, i, normed_product)
        if i >= 1:
            scatter_chips(0, i - 1)
    scatter_chips(0, chunks - 1)
    weight_grad(0, gath, hid_b, False)

    gain_term = jnp.zeros((1, channels), F32)
    bias_term = jnp.zeros((1, channels), F32)
    for i in range(chunks):
        value = scatter_finish(0, i)
        part = filt[i * step_h : (i + 1) * step_h].reshape(step, channels)
        centered = (part - mean) * rstd
        gain_term = gain_term + jnp.sum(value * centered, axis=0, keepdims=True)
        bias_term = bias_term + jnp.sum(value, axis=0, keepdims=True)
        dn[i * step_h : (i + 1) * step_h] = value.reshape(step_h, width, channels)
    mom_send[1] = jnp.zeros(mom_send.shape[1:], F32)
    mom_send[1, 0:1] = gain_term
    mom_send[1, 1:2] = bias_term
    moments_send(1)
    mom_recv[1, me_dp] = mom_send[1]
    for o in order:
        weight_issue(0, o)
    for i in range(chunks):
        scatter_sibling(1, i, branch_product)
        if i >= 1:
            scatter_chips(1, i - 1)
    scatter_chips(1, chunks - 1)
    for o in order:
        weight_stage(1, o)
    moments_wait(1)
    group_sum = [jnp.zeros(mom_send.shape[1:], F32) for _ in range(groups)]
    for d in range(n_dp):
        value = mom_recv[1, d]
        label = label_of(d)
        for g in range(groups):
            group_sum[g] = group_sum[g] + (label == g).astype(F32) * value
    own_sum = jnp.zeros(mom_send.shape[1:], F32)
    for g in range(groups):
        dgain_ref[g : g + 1] = group_sum[g][0:1]
        dbias_ref[g : g + 1] = group_sum[g][1:2]
        own_sum = own_sum + (mine == g).astype(F32) * group_sum[g]
    mean_gain, mean_bias = own_sum[0:1] / count, own_sum[1:2] / count
    factor = own_gain * rstd

    def load_row(r):
        centered = (filt[r] - mean) * rstd
        return factor * (dn[r] - mean_bias - centered * mean_gain)

    fill_shifts(height, width, load_row, shifts)
    lane_blocks = list(range(channels // LANE))
    ready = list(order)
    for lb in lane_blocks:
        conv_backward([lb], height, width, shifts, source, taps_in, filt, tap_sums)
        if len(ready) > 2:
            weight_stage(0, ready.pop(0))

    def finish_row(r, carry):
        din_ref[0, r] = (cot_ref[0, r].astype(F32) + filt[r]).astype(BF16)
        return carry

    lax.fori_loop(0, height, finish_row, 0)

    scale_sum = jnp.zeros((1, channels), F32)
    for i in range(chunks):
        branch = scatter_finish(1, i)
        cot = cot_ref[0, i * step_h : (i + 1) * step_h].reshape(step, channels).astype(F32)
        plain = source[i * step_h : (i + 1) * step_h].reshape(step, channels)
        scale_sum = scale_sum + jnp.sum(cot * branch, axis=0, keepdims=True)
        value = (plain + scale_ref[...] * branch).astype(BF16)
        result_ref[0, i * step_h : (i + 1) * step_h] = value.reshape(step_h, width, channels)

    n_taps = KS * KS
    pieces = hid // channels
    pack_y[me_y] = jnp.zeros(pack_y.shape[1:], F32)
    for tap in range(n_taps):
        pack_y[me_y, tap : tap + 1] = jnp.sum(tap_sums[tap], axis=0, keepdims=True)
    pack_y[me_y, n_taps : n_taps + 1] = scale_sum
    for p in range(pieces):
        pack_y[me_y, n_taps + 1 + p : n_taps + 2 + p] = bias_acc[
            0:1, p * channels : (p + 1) * channels
        ]
    for o in range(1, n_y):
        y = other(me_y, n_y, o)
        send(
            pack_y.at[me_y], pack_y.at[me_y], py_s.at[o], py_r.at[me_y], dp=me_z * n_y + y
        )

    while len(ready) > 1:
        weight_stage(0, ready.pop(0))
    for o in range(1, n_y):
        y = other(me_y, n_y, o)
        remote(
            pack_y.at[y], pack_y.at[y], py_s.at[o], py_r.at[y], dp=me_z * n_y + y
        ).wait_recv()
    pack = pack_y[0]
    for y in range(1, n_y):
        pack = pack + pack_y[y]
    pack_z[me_z] = pack
    for o in range(1, n_z):
        z = other(me_z, n_z, o)
        send(
            pack_z.at[me_z], pack_z.at[me_z], pz_s.at[o], pz_r.at[me_z], dp=z * n_y + me_y
        )
    for o in ready:
        weight_stage(0, o)

    for o in range(1, n_z):
        z = other(me_z, n_z, o)
        remote(
            pack_z.at[z], pack_z.at[z], pz_s.at[o], pz_r.at[z], dp=z * n_y + me_y
        ).wait_recv()
    pack = pack_z[0]
    for z in range(1, n_z):
        pack = pack + pack_z[z]
    dk_ref[...] = pack[:n_taps]
    dscale_ref[...] = pack[n_taps : n_taps + 1]
    for p in range(pieces):
        dbin_ref[0:1, p * channels : (p + 1) * channels] = pack[n_taps + 1 + p : n_taps + 2 + p]

    def weight_finish(t):
        value = z_send[t, 0].astype(F32)
        for o in range(1, n_z):
            z = other(me_z, n_z, o)
            remote(
                z_send.at[t, o], z_recv.at[t, z], wz_s.at[t, o], wz_r.at[t, z],
                dp=z * n_y + me_y,
            ).wait_recv()
            value = value + z_recv[t, z].astype(F32)
        return value

    dwout_ref[...] = weight_finish(1).T
    dwin_ref[...] = weight_finish(0)
    for copy in sends:
        copy.wait_send()


def body(n_dp, n_chan, activations, cotangent, dw_kernel, norm_gain, norm_bias, w_in, b_in, w_out,
         layer_scale, group_sizes):
    _, height, width, channels = activations.shape
    rows = height * width
    full = w_in.shape[0]
    hid = w_in.shape[1]
    groups = norm_gain.shape[0]
    chunks = 4
    n_x = n_chan // 2
    n_y = 1
    while n_dp % (2 * n_y) == 0 and 2 * (2 * n_y) ** 2 <= n_dp:
        n_y *= 2
    n_z = n_dp // n_y
    part = full // n_dp
    step = rows // chunks
    pack_rows = -(-(KS * KS + 1 + hid // channels) // 8) * 8
    vmem = pl.BlockSpec(memory_space=pltpu.VMEM)
    hbm = pl.BlockSpec(memory_space=pl.ANY)
    smem = pl.BlockSpec(memory_space=pltpu.SMEM)
    sds = jax.ShapeDtypeStruct
    dma = pltpu.SemaphoreType.DMA
    outs = pl.pallas_call(
        functools.partial(block_kernel, n_dp, n_y, n_chan, chunks),
        out_shape=(
            sds(activations.shape, BF16),
            sds(activations.shape, BF16),
            sds((KS * KS, channels), F32),
            sds((groups, channels), F32),
            sds((groups, channels), F32),
            sds((part, hid), F32),
            sds((1, hid), F32),
            sds((hid, part), F32),
            sds((1, channels), F32),
        ),
        in_specs=[smem, hbm, hbm, vmem, vmem, vmem, hbm, vmem, hbm, vmem],
        out_specs=(vmem,) * 9,
        scratch_shapes=[
            pltpu.VMEM(activations.shape, BF16),
            pltpu.VMEM(activations.shape, BF16),
            pltpu.VMEM(w_in.shape, BF16),
            pltpu.VMEM(w_out.shape, BF16),
            pltpu.VMEM((height, width, channels), F32),
            pltpu.VMEM((height, width, channels), F32),
            pltpu.VMEM((KS, height, width, channels), F32),
            pltpu.VMEM((KS * KS, SUB, channels), F32),
            pltpu.VMEM((n_chan, rows, channels), BF16),
            pltpu.VMEM((n_chan, rows, channels), BF16),
            pltpu.VMEM((rows, hid), F32),
            pltpu.VMEM((rows, hid), BF16),
            pltpu.VMEM((rows, hid), BF16),
            pltpu.VMEM((2, chunks, n_x, step, channels), BF16),
            pltpu.VMEM((2, chunks, n_x, step, channels), BF16),
            pltpu.VMEM((2, n_x, rows, channels), BF16),
            pltpu.VMEM((2, n_x, rows, channels), BF16),
            pltpu.VMEM((2, n_x, rows, channels), BF16),
            pltpu.VMEM((height, width, channels), F32),
            pltpu.VMEM((2, 8, channels), F32),
            pltpu.VMEM((2, n_dp, 8, channels), F32),
            pltpu.VMEM((2, n_dp, part, hid), BF16),
            pltpu.VMEM((2, n_y, n_z, part, hid), BF16),
            pltpu.VMEM((2, n_z, part, hid), BF16),
            pltpu.VMEM((2, n_z, part, hid), BF16),
            pltpu.VMEM((n_y, pack_rows, channels), F32),
            pltpu.VMEM((n_z, pack_rows, channels), F32),
            pltpu.VMEM((8, hid), F32),
            dma((4,)),
            dma((n_x, chunks + 1)),
            dma((n_x, chunks + 1)),
            dma((chunks + 1,)),
            dma((chunks + 1,)),
            dma((n_x, chunks + 1)),
            dma((n_x, chunks + 1)),
            dma((2, chunks)),
            dma((2, chunks)),
            dma((2, n_x, chunks)),
            dma((2, n_x, chunks)),
            dma((2, n_dp)),
            dma((2, n_dp)),
            dma((2, n_y, n_z)),
            dma((2, n_y, n_z)),
            dma((2, n_z)),
            dma((2, n_z)),
            dma((n_y,)),
            dma((n_y,)),
            dma((n_z,)),
            dma((n_z,)),
        ],
        compiler_params=pltpu.CompilerParams(
            collective_id=0, has_side_effects=True, vmem_limit_bytes=60 * 1024 * 1024
        ),
    )(
        group_sizes, activations, cotangent, dw_kernel, norm_gain, norm_bias, w_in,
        b_in[None], w_out, layer_scale[None],
    )
    result, d_input, d_kernel, d_gain, d_bias, d_w_in, d_b_in, d_w_out, d_scale = outs
    return (result, d_input, d_kernel, d_gain, d_bias, d_w_in, d_b_in[0], d_w_out, d_scale[0])


def solution(mesh):
    step = functools.partial(body, mesh.shape["dp"], mesh.shape["chan"])
    in_specs = (
        P("dp", None, None, "chan"),
        P("dp", None, None, "chan"),
        P(None, "chan"),
        P(None, "chan"),
        P(None, "chan"),
        P(None, "chan"),
        P("chan"),
        P("chan", None),
        P("chan"),
        P(),
    )
    out_specs = (
        P("dp", None, None, "chan"),
        P("dp", None, None, "chan"),
        P(None, "chan"),
        P(None, "chan"),
        P(None, "chan"),
        P("dp", "chan"),
        P("chan"),
        P("chan", "dp"),
        P("chan"),
    )
    return jax.shard_map(step, mesh=mesh, in_specs=in_specs, out_specs=out_specs, check_vma=False)
```
